512 devices in a mesh: win: 64 (over z, x), rcv: 8 (over y, core).
Axes of the slice: x: 4, y: 4, z: 16, core: 2. Of those that a mesh axis runs over, the one named last changes fastest.
Arguments:
- spectra: bfloat16 [128, 2, 128, 4096], P('win', None, 'rcv'), may hold values from -6 to 6
- source_channel: int32 [8], replicated, may hold values from 0 to 127
Outputs:
- stack: float32 [512, 8, 128], P('win', None, 'rcv')
The draws below stay inside these ranges and needn't reach their ends.
All inputs are finite; a program needn't handle non-finite values.
Results may differ from the reference program's by a relative error of at most 0.0011.
Values may be sent and summed in bfloat16 or wider, within the bound.
A program may use at most 64 MiB of HBM per device.

```python
import jax
import jax.numpy as jnp
from jax import lax

F = 4096
L = 512
S = 8
ITERS = 5
R = 128
W = 128


def touch_ends(array, key, low, top_value):
    longest = array.shape.index(max(array.shape))
    spots = []
    for shift in (0, 1):
        where = [jax.random.randint(jax.random.fold_in(key, axis), (), 0, length) for axis, length in enumerate(array.shape)]
        where[longest] = (where[longest] + shift) % array.shape[longest]
        spots.append(tuple(where))
    return array.at[spots[0]].set(low).at[spots[1]].set(top_value)


def shard_levels(stream_key, dims, shards, smallest, top_value):
    def one(dim, parts):
        steps = jax.random.uniform(jax.random.fold_in(jax.random.fold_in(stream_key, 6), dim), (parts,), jnp.float32, smallest / len(shards), top_value / len(shards))
        return jnp.repeat(jnp.exp(steps), dims[dim] // parts).reshape((-1,) + (1,) * (len(dims) - dim - 1))

    level = one(*shards[0])
    for cut in shards[1:]:
        level = level * one(*cut)
    return level


def centred(own_key, extent, width, reach, shards=(), kind=jnp.bfloat16):
    entries = jax.random.normal(own_key, extent, jnp.float32) * width
    if len(shards) > 0:
        entries = shard_levels(own_key, extent, shards, -0.22, 0.18) * entries
    return jnp.clip(entries, min=-reach, max=reach).astype(kind)


def setup_inputs(seed: int = 0) -> dict:
    key_list = jax.random.split(jax.random.key(seed), 3)
    return {
        "spectra": centred(key_list[0], (W, 2, R, F), 1.0, 6.0, ((0, 64), (2, 8))),
        "source_channel": touch_ends(jax.random.randint(key_list[1], (S,), 0, R), jax.random.fold_in(key_list[1], 1), 0, R - 1).astype(jnp.int32),
    }


TUKEY = 4.685
EPSILON = 1e-06

def make_basis(bin_count, lag_count):
    freq = jnp.arange(bin_count, dtype=jnp.int32)
    shifts = jnp.arange(lag_count, dtype=jnp.int32) - lag_count // 2
    phase = shifts[:, None] * freq[None, :] % (2 * bin_count)
    angle = phase.astype(jnp.float32) * (2.0 * jnp.pi / (2 * bin_count))
    factor = jnp.where(freq == 0, 1.0, 2.0).astype(jnp.float32) / jnp.sqrt(jnp.float32(8 * bin_count))
    table = jnp.concatenate([jnp.cos(angle) * factor[None, :], -jnp.sin(angle) * factor[None, :]], axis=1)
    return table.astype(jnp.bfloat16)

def bisquare_stack(samples):
    center = lax.optimization_barrier(jnp.mean(samples, axis=0))
    for iteration in range(ITERS):
        deviation = samples - center
        squared = deviation * deviation
        scale_two = lax.optimization_barrier(jnp.mean(squared, axis=0)) + EPSILON
        ratio = squared / (TUKEY * TUKEY * scale_two)
        weight = jnp.where(ratio < 1.0, (1.0 - ratio) * (1.0 - ratio), 0.0)
        center = lax.optimization_barrier(jnp.sum(weight * samples, axis=0)) / lax.optimization_barrier(jnp.sum(weight, axis=0))
    return center

def reference(spectra, source_channel):
    basis = make_basis(F, L)

    def one_window(window):
        picked = window[:, source_channel, :].astype(jnp.float32)
        receivers = window.astype(jnp.float32)
        real_a = picked[0][:, None, :]
        imag_b = picked[1][:, None, :]
        real_p = receivers[0][None, :, :]
        imag_q = receivers[1][None, :, :]
        real_part = (real_a * real_p + imag_b * imag_q).reshape(S * R, F)
        imag_part = (imag_b * real_p - real_a * imag_q).reshape(S * R, F)
        cross = jnp.concatenate([real_part, imag_part], axis=1).astype(jnp.bfloat16)
        return jnp.dot(basis, cross.T, preferred_element_type=jnp.float32)
    corr = lax.map(one_window, spectra)
    return bisquare_stack(corr).reshape(L, S, R)
```

```python
import jax
import jax.numpy as jnp
from jax import lax
from jax.experimental import pallas as pl
from jax.experimental.pallas import tpu as pltpu
from jax.sharding import PartitionSpec as P

L = 512
ITERS = 5
TUKEY = 4.685
EPSILON = 1e-06
MESH = pl.DeviceIdType.MESH
NZ, NX = 16, 4
WIN = NZ * NX
BLOCK = L // WIN


def signed(step, count):
    return step if step <= count // 2 else step - count


def offsets():
    found = [(dz, dx) for dz in range(NZ) for dx in range(NX) if dz or dx]
    return sorted(found, key=lambda o: -(4 * abs(signed(o[0], NZ)) + abs(signed(o[1], NX))))


def tables(shifts, bins, total):
    angle = (shifts[:, None] * bins[None, :] % total).astype(jnp.float32) * (2.0 * jnp.pi / total)
    return jnp.cos(angle), jnp.sin(angle)


def make_basis(bin_count):
    freq = jnp.arange(bin_count, dtype=jnp.int32)
    total = 2 * bin_count
    factor = jnp.where(freq == 0, 1.0, 2.0).astype(jnp.float32) / jnp.sqrt(jnp.float32(4 * total))
    coarse_c, coarse_s = tables(jnp.arange(32, dtype=jnp.int32) * 16 - L // 2, freq, total)
    fine_c, fine_s = tables(jnp.arange(16, dtype=jnp.int32), freq, total)
    coarse_c, coarse_s, fine_c, fine_s = lax.optimization_barrier((coarse_c * factor, coarse_s * factor, fine_c, fine_s))
    cos = coarse_c[:, None] * fine_c[None] - coarse_s[:, None] * fine_s[None]
    sin = coarse_s[:, None] * fine_c[None] + coarse_c[:, None] * fine_s[None]
    return cos.astype(jnp.bfloat16).reshape(L, bin_count), (-sin).astype(jnp.bfloat16).reshape(L, bin_count)


def stack_kernel(x_ref, o_ref, got, vals, send_sem, recv_sem):
    me = lax.axis_index("win")
    z, x = me // NX, lax.rem(me, NX)
    peers = [lax.rem(z + dz, NZ) * NX + lax.rem(x + dx, NX) for dz, dx in offsets()]
    barrier = pltpu.get_barrier_semaphore()
    for peer in peers:
        pl.semaphore_signal(barrier, inc=1, device_id={"win": peer}, device_id_type=MESH)
    pl.semaphore_wait(barrier, WIN - 1)
    for peer in peers:
        pltpu.make_async_remote_copy(
            x_ref.at[peer], got.at[me], send_sem, recv_sem, device_id={"win": peer}, device_id_type=MESH
        ).start()
    got[me] = x_ref[me]
    pltpu.make_async_copy(got.at[pl.ds(0, WIN - 1)], got.at[pl.ds(0, WIN - 1)], recv_sem).wait()
    windows = 2 * WIN
    sums = [None] * 8
    for w in range(windows):
        value = got[w // 2, pl.ds(BLOCK * (w % 2), BLOCK), :].astype(jnp.float32) * (1.0 / (1.0 + w / 128.0))
        vals[w] = value
        sums[w % 8] = value if sums[w % 8] is None else sums[w % 8] + value
    total = sum(sums[1:], sums[0])
    mean = total * (1.0 / windows)
    sums = [jnp.zeros_like(mean)] * 8
    for w in range(windows):
        dev = vals[w] - mean
        sums[w % 8] = sums[w % 8] + dev * dev
    var = sum(sums[1:], sums[0]) * (1.0 / windows)
    center = mean
    for _ in range(ITERS):
        shift = mean - center
        inverse = 1.0 / (TUKEY * TUKEY * (var + shift * shift + EPSILON))
        weights = [jnp.zeros_like(mean)] * 8
        moved = [jnp.zeros_like(mean)] * 8
        for w in range(windows):
            dev = vals[w] - center
            root = jnp.maximum(1.0 - dev * dev * inverse, 0.0)
            weight = root * root
            weights[w % 8] = weights[w % 8] + weight
            moved[w % 8] = moved[w % 8] + weight * dev
        center = center + sum(moved[1:], moved[0]) / sum(weights[1:], weights[0])
    o_ref[...] = center
    pltpu.make_async_copy(x_ref.at[pl.ds(0, WIN - 1)], x_ref.at[pl.ds(0, WIN - 1)], send_sem).wait()


def exchange_and_stack(blocks):
    return pl.pallas_call(
        stack_kernel,
        out_shape=jax.ShapeDtypeStruct((BLOCK, 128), jnp.float32),
        in_specs=[pl.BlockSpec(memory_space=pltpu.VMEM)],
        out_specs=pl.BlockSpec(memory_space=pltpu.VMEM),
        scratch_shapes=[
            pltpu.VMEM((WIN, 2 * BLOCK, 128), jnp.bfloat16),
            pltpu.VMEM((2 * WIN, BLOCK, 128), jnp.float32),
            pltpu.SemaphoreType.DMA,
            pltpu.SemaphoreType.DMA,
        ],
        compiler_params=pltpu.CompilerParams(collective_id=0, has_side_effects=True),
    )(blocks)


def per_device(spectra, source_channel):
    win_count, _, chan_count, bin_count = spectra.shape
    source_count = source_channel.shape[0]
    channels = lax.axis_index("rcv") * chan_count + lax.iota(jnp.int32, chan_count)
    onehot = (source_channel[:, None] == channels[None, :]).astype(jnp.bfloat16)
    own_part = jnp.einsum("sr,wcrf->wcsf", onehot, spectra, preferred_element_type=jnp.float32).astype(jnp.bfloat16)
    parts = lax.all_to_all(jnp.broadcast_to(own_part[None], (8, *own_part.shape)), "rcv", 0, 0, tiled=True)
    source_float = parts.astype(jnp.float32).sum(axis=0)
    receiver_float = spectra.astype(jnp.float32)
    real_a = source_float[:, 0][:, :, None, :]
    imag_b = source_float[:, 1][:, :, None, :]
    real_p = receiver_float[:, 0][:, None, :, :]
    imag_q = receiver_float[:, 1][:, None, :, :]
    pair_count = source_count * chan_count
    real_part = (real_a * real_p + imag_b * imag_q).reshape(win_count, pair_count, bin_count).astype(jnp.bfloat16)
    imag_part = (imag_b * real_p - real_a * imag_q).reshape(win_count, pair_count, bin_count).astype(jnp.bfloat16)
    cos, sin = make_basis(bin_count)
    corr = jnp.einsum("lk,wpk->lwp", cos, real_part, preferred_element_type=jnp.float32)
    corr = corr + jnp.einsum("lk,wpk->lwp", sin, imag_part, preferred_element_type=jnp.float32)
    window = 2 * lax.axis_index("win") + lax.iota(jnp.int32, 2)
    scaled = corr * (1.0 + window.astype(jnp.float32) / 128.0)[None, :, None]
    blocks = scaled.astype(jnp.bfloat16).reshape(WIN, BLOCK, 2, pair_count).transpose(0, 2, 1, 3)
    result = exchange_and_stack(blocks.reshape(WIN, 2 * BLOCK, pair_count))
    return result.reshape(BLOCK, source_count, chan_count)


def solution(mesh):
    return jax.shard_map(
        per_device,
        mesh=mesh,
        in_specs=(P("win", None, "rcv", None), P()),
        out_specs=P("win", None, "rcv"),
        check_vma=False,
    )
```

```python
import jax
import jax.numpy as jnp
from jax import lax
from jax.experimental import pallas as pl
from jax.experimental.pallas import tpu as pltpu
from jax.sharding import PartitionSpec as P

L = 512
F = 4096
ITERS = 5
TUKEY = 4.685
EPSILON = 1e-06
MESH = pl.DeviceIdType.MESH
NZ, NX, NY = 16, 4, 4
WIN = NZ * NX
BLOCK = L // WIN
HALF = L // 2
ROWS = HALF + 16
QUARTER = F // NY
COLS = 512
PAIRS = 128


def signed(step, count):
    return step if step <= count // 2 else step - count


def offsets():
    found = [(dz, dx) for dz in range(NZ) for dx in range(NX) if dz or dx]
    return sorted(found, key=lambda o: -(4 * abs(signed(o[0], NZ)) + abs(signed(o[1], NX))))


def cos_sin(phase):
    turn = (phase + 1024) >> 11
    x = (phase - (turn << 11)).astype(jnp.float32) * (2.0 * jnp.pi / (2 * F))
    y = x * x
    s = x * (1.0 + y * (-1.0 / 6 + y * (1.0 / 120 + y * (-1.0 / 5040 + y * (1.0 / 362880)))))
    c = 1.0 + y * (-0.5 + y * (1.0 / 24 + y * (-1.0 / 720 + y * (1.0 / 40320))))
    odd = (turn & 1) == 1
    cos = jnp.where(odd, s, c)
    sin = jnp.where(odd, c, s)
    cos = jnp.where(((turn + 1) & 2) == 2, -cos, cos)
    sin = jnp.where((turn & 2) == 2, -sin, sin)
    return cos, sin


def fill_table(cos_ref, sin_ref, rows, step, scaled):
    for part in range(F // COLS):
        cols = pl.ds(part * COLS, COLS)
        freq = part * COLS + lax.broadcasted_iota(jnp.int32, (rows, COLS), 1)
        row = lax.broadcasted_iota(jnp.int32, (rows, COLS), 0)
        cos, sin = cos_sin((row * freq * step) & (2 * F - 1))
        if scaled:
            factor = jnp.where(freq == 0, 1.0, 2.0) * (1.0 / (8 * F) ** 0.5)
            cos, sin = cos * factor, sin * factor
        cos_ref[:, cols] = cos
        sin_ref[:, cols] = sin


def fill_basis(first, last, coarse_c, coarse_s, fine_c, fine_s, basis_c, basis_s):
    for part in range(F // COLS):
        cols = pl.ds(part * COLS, COLS)
        quarter, start = divmod(part * COLS, QUARTER)
        fc, fs = fine_c[:, cols], fine_s[:, cols]

        def one(g, _, cols=cols, quarter=quarter, start=start, fc=fc, fs=fs):
            cc, cs = coarse_c[pl.ds(g, 1), cols], coarse_s[pl.ds(g, 1), cols]
            rows = pl.ds(pl.multiple_of(g * 16, 16), 16)
            basis_c[quarter, rows, start : start + COLS] = (cc * fc - cs * fs).astype(jnp.bfloat16)
            basis_s[quarter, rows, start : start + COLS] = (-(cs * fc) - cc * fs).astype(jnp.bfloat16)
            return 0

        lax.fori_loop(first, last, one, 0)


def stack(got, vals):
    windows = 2 * WIN
    sums = [None] * 8
    for w in range(windows):
        value = got[w // 2, pl.ds(BLOCK * (w % 2), BLOCK), :].astype(jnp.float32) * (1.0 / (1.0 + w / 128.0))
        vals[w] = value
        sums[w % 8] = value if sums[w % 8] is None else sums[w % 8] + value
    total = sum(sums[1:], sums[0])
    mean = total * (1.0 / windows)
    sums = [jnp.zeros_like(mean)] * 8
    for w in range(windows):
        dev = vals[w] - mean
        sums[w % 8] = sums[w % 8] + dev * dev
    var = sum(sums[1:], sums[0]) * (1.0 / windows)
    center = mean
    for _ in range(ITERS):
        shift = mean - center
        inverse = 1.0 / (TUKEY * TUKEY * (var + shift * shift + EPSILON))
        weights = [jnp.zeros_like(mean)] * 8
        moved = [jnp.zeros_like(mean)] * 8
        for w in range(windows):
            dev = vals[w] - center
            root = jnp.maximum(1.0 - dev * dev * inverse, 0.0)
            weight = root * root
            weights[w % 8] = weights[w % 8] + weight
            moved[w % 8] = moved[w % 8] + weight * dev
        center = center + sum(moved[1:], moved[0]) / sum(weights[1:], weights[0])
    return center


def remote(src, dst, send_sem, recv_sem, where):
    return pltpu.make_async_remote_copy(src, dst, send_sem, recv_sem, device_id=where, device_id_type=MESH)


def wait_bytes(ref, sem):
    pltpu.make_async_copy(ref, ref, sem).wait()


def kernel(
    channel_ref, spectra_ref, o_ref,
    spec, own, pair, summed, parts, sources, source_f,
    coarse_c, coarse_s, fine_c, fine_s, basis_c, basis_s, cross_r, cross_i, acc_c, acc_s,
    blocks, got, vals,
    spec_sem, pair_s, pair_r, part_s, part_r, all_s, all_r, to_s, to_r, send_s, send_r,
):
    me = lax.axis_index("win")
    z, x = me // NX, lax.rem(me, NX)
    mine = lax.axis_index("rcv")
    y, core = mine // 2, lax.rem(mine, 2)
    other = 1 - core
    peers = [lax.rem(z + dz, NZ) * NX + lax.rem(x + dx, NX) for dz, dx in offsets()]
    partner = {"rcv": 2 * y + other}
    across = {d: {"rcv": 2 * lax.rem(y + d, NY) + core} for d in (1, 2, 3)}
    quarter = {d: lax.rem(y + NY - d, NY) for d in range(NY)}

    loads = [
        pltpu.make_async_copy(spectra_ref.at[:, :, :, pl.ds(q * QUARTER, QUARTER)], spec.at[q], spec_sem.at[q])
        for q in range(NY)
    ]
    for load in loads:
        load.start()
    barrier = pltpu.get_barrier_semaphore()
    for d in range(1, 8):
        pl.semaphore_signal(barrier, inc=1, device_id={"rcv": lax.rem(mine + d, 8)}, device_id_type=MESH)
    for peer in peers:
        pl.semaphore_signal(barrier, inc=1, device_id={"win": peer}, device_id_type=MESH)

    fill_table(fine_c, fine_s, 16, 1, False)
    for load in loads:
        load.wait()
    row = lax.broadcasted_iota(jnp.int32, (16, 16), 0)
    column = lax.broadcasted_iota(jnp.int32, (16, 16), 1) + mine * 16
    onehot = jnp.zeros((16, 16), jnp.float32)
    for s in range(8):
        onehot = jnp.where((row == s) & (column == channel_ref[s]), 1.0, onehot)
    onehot = onehot.astype(jnp.bfloat16)
    for w in range(2):
        for q in range(NY):
            picked = [
                jnp.dot(onehot, spec[q, w, c], preferred_element_type=jnp.float32)[:8] for c in range(2)
            ]
            own[w, q] = jnp.concatenate(picked, axis=0).astype(jnp.bfloat16)
    pl.semaphore_wait(barrier, 7 + WIN - 1)

    swap = remote(own.at[other], pair, pair_s, pair_r, partner)
    swap.start()
    fill_table(coarse_c, coarse_s, 24, 16, True)
    swap.wait_recv()
    for q in range(NY):
        summed[q] = own[core, q] + pair[q]
    scatter = [
        remote(summed.at[lax.rem(y + d, NY)], parts.at[d - 1], part_s, part_r, across[d]) for d in (2, 1, 3)
    ]
    for copy in scatter:
        copy.start()
    fill_basis(0, ROWS // 16, coarse_c, coarse_s, fine_c, fine_s, basis_c, basis_s)
    wait_bytes(parts, part_r)
    sources[core, y] = summed[y] + parts[0] + parts[1] + parts[2]
    held = sources.at[core, y]
    gather = {d: remote(held, held, all_s, all_r.at[d - 1], across[d]) for d in (2, 1, 3)}
    for d in (2, 1, 3):
        gather[d].start()

    def hand(d):
        there = sources.at[core, quarter[d]]
        copy = remote(there, there, to_s, to_r.at[d], partner)
        copy.start()
        return copy

    def compute(d):
        q = quarter[d]
        hands[d].wait_recv()
        for w in range(2):
            source_f[w] = sources[w, q].astype(jnp.float32)
        for w in range(2):
            for part in range(QUARTER // COLS):
                cols = pl.ds(part * COLS, COLS)
                p = spec[q, w, 0, :, cols].astype(jnp.float32)
                i = spec[q, w, 1, :, cols].astype(jnp.float32)
                for s in range(8):
                    a = source_f[w, pl.ds(s, 1), cols]
                    b = source_f[w, pl.ds(8 + s, 1), cols]
                    rows = pl.ds(w * PAIRS + s * 16, 16)
                    cross_r[d, rows, cols] = (a * p + b * i).astype(jnp.bfloat16)
                    cross_i[d, rows, cols] = (b * p - a * i).astype(jnp.bfloat16)
        dims = (((1,), (1,)), ((), ()))
        sum_c = lax.dot_general(basis_c[q], cross_r[d], dims, preferred_element_type=jnp.float32)
        sum_s = lax.dot_general(basis_s[q], cross_i[d], dims, preferred_element_type=jnp.float32)
        if d == 0:
            acc_c[...] = sum_c
            acc_s[...] = sum_s
        else:
            acc_c[...] += sum_c
            acc_s[...] += sum_s

    hands = {0: hand(0)}
    compute(0)
    for d in (1, 3, 2):
        gather[d].wait_recv()
        hands[d] = hand(d)
    for d in (1, 3, 2):
        compute(d)

    window = (2 * me).astype(jnp.float32)
    scales = [1.0 + (window + w) * (1.0 / 128.0) for w in range(2)]
    for ahead in (True, False):
        first = 0 if ahead else 1
        c, s = acc_c[pl.ds(first, HALF), :], acc_s[pl.ds(first, HALF), :]
        lags = c + s if ahead else c - s
        halves = [(lags[:, w * PAIRS : (w + 1) * PAIRS] * scales[w]).reshape(32, BLOCK, PAIRS) for w in range(2)]
        both = jnp.concatenate(halves, axis=1).astype(jnp.bfloat16)
        if ahead:
            blocks[pl.ds(32, 32)] = both
        else:
            for m in range(32):
                blocks[31 - m] = both[m]
    for peer in peers:
        remote(blocks.at[peer], got.at[me], send_s, send_r, {"win": peer}).start()
    got[me] = blocks[me]
    wait_bytes(got.at[pl.ds(0, WIN - 1)], send_r)
    center = stack(got, vals)

    @pl.when(me >= 32)
    def _():
        o_ref[...] = center

    @pl.when(me < 32)
    def _():
        for k in range(BLOCK):
            o_ref[pl.ds(BLOCK - 1 - k, 1), :] = center[k : k + 1]

    swap.wait_send()
    wait_bytes(parts, part_s)
    wait_bytes(parts, all_s)
    wait_bytes(sources.at[0], to_s)
    wait_bytes(blocks.at[pl.ds(0, WIN - 1)], send_s)


def per_device(spectra, source_channel):
    bf, f32, dma = jnp.bfloat16, jnp.float32, pltpu.SemaphoreType.DMA
    result = pl.pallas_call(
        kernel,
        out_shape=jax.ShapeDtypeStruct((BLOCK, PAIRS), f32),
        in_specs=[pl.BlockSpec(memory_space=pltpu.SMEM), pl.BlockSpec(memory_space=pl.ANY)],
        out_specs=pl.BlockSpec(memory_space=pltpu.VMEM),
        scratch_shapes=[
            pltpu.VMEM((NY, 2, 2, 16, QUARTER), bf),
            pltpu.VMEM((2, NY, 16, QUARTER), bf),
            pltpu.VMEM((NY, 16, QUARTER), bf),
            pltpu.VMEM((NY, 16, QUARTER), bf),
            pltpu.VMEM((NY - 1, 16, QUARTER), bf),
            pltpu.VMEM((2, NY, 16, QUARTER), bf),
            pltpu.VMEM((2, 16, QUARTER), f32),
            pltpu.VMEM((24, F), f32),
            pltpu.VMEM((24, F), f32),
            pltpu.VMEM((16, F), f32),
            pltpu.VMEM((16, F), f32),
            pltpu.VMEM((NY, ROWS, QUARTER), bf),
            pltpu.VMEM((NY, ROWS, QUARTER), bf),
            pltpu.VMEM((NY, 2 * PAIRS, QUARTER), bf),
            pltpu.VMEM((NY, 2 * PAIRS, QUARTER), bf),
            pltpu.VMEM((ROWS, 2 * PAIRS), f32),
            pltpu.VMEM((ROWS, 2 * PAIRS), f32),
            pltpu.VMEM((WIN, 2 * BLOCK, PAIRS), bf),
            pltpu.VMEM((WIN, 2 * BLOCK, PAIRS), bf),
            pltpu.VMEM((2 * WIN, BLOCK, PAIRS), f32),
            dma((NY,)), dma, dma, dma, dma, dma, dma((NY - 1,)), dma, dma((NY,)), dma, dma,
        ],
        compiler_params=pltpu.CompilerParams(
            collective_id=0, has_side_effects=True, vmem_limit_bytes=40 * 1024 * 1024
        ),
    )(source_channel, spectra)
    return result.reshape(BLOCK, 8, 16)


def solution(mesh):
    return jax.shard_map(
        per_device,
        mesh=mesh,
        in_specs=(P("win", None, "rcv", None), P()),
        out_specs=P("win", None, "rcv"),
        check_vma=False,
    )
```

```python
import jax
import jax.numpy as jnp
from jax import lax
from jax.experimental import pallas as pl
from jax.experimental.pallas import tpu as pltpu
from jax.sharding import PartitionSpec as P

L = 512
F = 4096
ITERS = 5
TUKEY = 4.685
EPSILON = 1e-06
MESH = pl.DeviceIdType.MESH
NZ, NX, NY = 16, 4, 4
WIN = NZ * NX
BLOCK = L // WIN
HALF = L // 2
ROWS = HALF + 16
QUARTER = F // NY
COLS = 512
PAIRS = 128


def signed(step, count):
    return step if step <= count // 2 else step - count


def offsets():
    found = [(dz, dx) for dz in range(NZ) for dx in range(NX) if dz or dx]
    return sorted(found, key=lambda o: -(4 * abs(signed(o[0], NZ)) + abs(signed(o[1], NX))))


def cos_sin(phase):
    turn = (phase + 1024) >> 11
    x = (phase - (turn << 11)).astype(jnp.float32) * (2.0 * jnp.pi / (2 * F))
    y = x * x
    s = x * (1.0 + y * (-1.0 / 6 + y * (1.0 / 120 + y * (-1.0 / 5040 + y * (1.0 / 362880)))))
    c = 1.0 + y * (-0.5 + y * (1.0 / 24 + y * (-1.0 / 720 + y * (1.0 / 40320))))
    odd = (turn & 1) == 1
    cos = jnp.where(odd, s, c)
    sin = jnp.where(odd, c, s)
    cos = jnp.where(((turn + 1) & 2) == 2, -cos, cos)
    sin = jnp.where((turn & 2) == 2, -sin, sin)
    return cos, sin


def fill_table(cos_ref, sin_ref, rows, step, scaled):
    for part in range(F // COLS):
        cols = pl.ds(part * COLS, COLS)
        freq = part * COLS + lax.broadcasted_iota(jnp.int32, (rows, COLS), 1)
        row = lax.broadcasted_iota(jnp.int32, (rows, COLS), 0)
        cos, sin = cos_sin((row * freq * step) & (2 * F - 1))
        if scaled:
            factor = jnp.where(freq == 0, 1.0, 2.0) * (1.0 / (8 * F) ** 0.5)
            cos, sin = cos * factor, sin * factor
        cos_ref[:, cols] = cos
        sin_ref[:, cols] = sin


def fill_basis(first, last, coarse_c, coarse_s, fine_c, fine_s, basis_c, basis_s):
    for part in range(F // COLS):
        cols = pl.ds(part * COLS, COLS)
        quarter, start = divmod(part * COLS, QUARTER)
        fc, fs = fine_c[:, cols], fine_s[:, cols]

        def one(g, _, cols=cols, quarter=quarter, start=start, fc=fc, fs=fs):
            cc, cs = coarse_c[pl.ds(g, 1), cols], coarse_s[pl.ds(g, 1), cols]
            rows = pl.ds(pl.multiple_of(g * 16, 16), 16)
            basis_c[quarter, rows, start : start + COLS] = (cc * fc - cs * fs).astype(jnp.bfloat16)
            basis_s[quarter, rows, start : start + COLS] = (-(cs * fc) - cc * fs).astype(jnp.bfloat16)
            return 0

        lax.fori_loop(first, last, one, 0)


def stack(got, vals):
    windows = 2 * WIN
    sums = [None] * 8
    for w in range(windows):
        value = got[w // 2, pl.ds(BLOCK * (w % 2), BLOCK), :].astype(jnp.float32) * (1.0 / (1.0 + w / 128.0))
        vals[w] = value
        sums[w % 8] = value if sums[w % 8] is None else sums[w % 8] + value
    total = sum(sums[1:], sums[0])
    mean = total * (1.0 / windows)
    sums = [jnp.zeros_like(mean)] * 8
    for w in range(windows):
        dev = vals[w] - mean
        sums[w % 8] = sums[w % 8] + dev * dev
    var = sum(sums[1:], sums[0]) * (1.0 / windows)
    center = mean
    for _ in range(ITERS):
        shift = mean - center
        inverse = 1.0 / (TUKEY * TUKEY * (var + shift * shift + EPSILON))
        weights = [jnp.zeros_like(mean)] * 8
        moved = [jnp.zeros_like(mean)] * 8
        for w in range(windows):
            dev = vals[w] - center
            root = jnp.maximum(1.0 - dev * dev * inverse, 0.0)
            weight = root * root
            weights[w % 8] = weights[w % 8] + weight
            moved[w % 8] = moved[w % 8] + weight * dev
        center = center + sum(moved[1:], moved[0]) / sum(weights[1:], weights[0])
    return center


def remote(src, dst, send_sem, recv_sem, where):
    return pltpu.make_async_remote_copy(src, dst, send_sem, recv_sem, device_id=where, device_id_type=MESH)


def wait_bytes(ref, sem):
    pltpu.make_async_copy(ref, ref, sem).wait()


ORDER = (0, 2, 1, 3)


def kernel(
    channel_hbm, spectra_ref, o_ref,
    channel_ref, spec, own, pair, first, got1, second, got2, sources, source_f,
    coarse_c, coarse_s, fine_c, fine_s, basis_c, basis_s, cross_r, cross_i, acc_c, acc_s,
    blocks, got, vals,
    chan_sem, spec_sem, pair_s, pair_r, one_s, one_r, two_s, two_r, to_s, to_r, send_s, send_r, near, mid, far,
):
    me = lax.axis_index("win")
    z, x = me // NX, lax.rem(me, NX)
    mine = lax.axis_index("rcv")
    y, core = mine // 2, lax.rem(mine, 2)
    other = 1 - core
    peers = [lax.rem(z + dz, NZ) * NX + lax.rem(x + dx, NX) for dz, dx in offsets()]
    partner = {"rcv": 2 * y + other}
    left = {"rcv": 2 * (y + 1 - 2 * lax.rem(y, 2)) + core}
    right = {"rcv": 2 * (NY - 1 - y) + core}

    def along(dz):
        return {"win": lax.rem(z + NZ + dz, NZ) * NX + x}

    loads = {
        q: pltpu.make_async_copy(spectra_ref.at[:, :, :, pl.ds(q * QUARTER, QUARTER)], spec.at[q], spec_sem.at[q])
        for q in ORDER
    }
    for q in ORDER:
        loads[q].start()
    channels = pltpu.make_async_copy(channel_hbm, channel_ref, chan_sem)
    channels.start()
    barrier = pltpu.get_barrier_semaphore()
    greeted = 0
    for d in range(1, 8):
        pl.semaphore_signal(barrier, inc=1, device_id={"rcv": lax.rem(mine + d, 8)}, device_id_type=MESH)
        greeted += 1
    for dz in (-1, 0, 1):
        for dx in range(NX):
            if dz or dx:
                where = {"win": lax.rem(z + NZ + dz, NZ) * NX + lax.rem(x + dx, NX)}
                pl.semaphore_signal(barrier, inc=1, device_id=where, device_id_type=MESH)
                greeted += 1

    fill_table(fine_c, fine_s, 16, 1, False)
    fill_table(coarse_c, coarse_s, 24, 16, True)
    channels.wait()
    row = lax.broadcasted_iota(jnp.int32, (16, 16), 0)
    column = lax.broadcasted_iota(jnp.int32, (16, 16), 1) + mine * 16
    onehot = jnp.zeros((16, 16), jnp.float32)
    for s in range(8):
        onehot = jnp.where((row == s) & (column == channel_ref[s]), 1.0, onehot)
    onehot = onehot.astype(jnp.bfloat16)
    for q in ORDER:
        loads[q].wait()
    for w in range(2):
        for q in range(NY):
            picked = [
                jnp.dot(onehot, spec[q, w, c], preferred_element_type=jnp.float32)[:8] for c in range(2)
            ]
            own[w, q] = jnp.concatenate(picked, axis=0).astype(jnp.bfloat16)
    pl.semaphore_wait(barrier, greeted)

    for dz in (-1, 1):
        pl.semaphore_signal(near, inc=1, device_id=along(dz), device_id_type=MESH)

    swap = {q: remote(own.at[other, q], pair.at[q], pair_s, pair_r.at[q], partner) for q in ORDER}
    for q in ORDER:
        swap[q].start()
    one = {q: remote(first.at[q], got1.at[q], one_s, one_r.at[q], left if q < 2 else right) for q in ORDER}
    two = {q: remote(second.at[q], got2.at[q], two_s, two_r.at[q], right if q < 2 else left) for q in ORDER}
    hand = {q: remote(sources.at[core, q], sources.at[core, q], to_s, to_r.at[q], partner) for q in ORDER}
    for q in ORDER:
        swap[q].wait_recv()
        first[q] = own[core, q] + pair[q]
        one[q].start()
    pl.semaphore_wait(near, 2)
    for dz in (-2, 2):
        pl.semaphore_signal(mid, inc=1, device_id=along(dz), device_id_type=MESH)
    fill_basis(0, ROWS // 16, coarse_c, coarse_s, fine_c, fine_s, basis_c, basis_s)
    for q in ORDER:
        one[q].wait_recv()
        second[q] = first[q] + got1[q]
        two[q].start()
    pl.semaphore_wait(mid, 2)
    for dz in (-4, 4):
        pl.semaphore_signal(far, inc=1, device_id=along(dz), device_id_type=MESH)

    def cross(q, at):
        w = other if at else core
        source_f[at] = sources[w, q].astype(jnp.float32)
        for part in range(QUARTER // COLS):
            cols = pl.ds(part * COLS, COLS)
            p = spec[q, w, 0, :, cols].astype(jnp.float32)
            i = spec[q, w, 1, :, cols].astype(jnp.float32)
            for s in range(8):
                a = source_f[at, pl.ds(s, 1), cols]
                b = source_f[at, pl.ds(8 + s, 1), cols]
                rows = pl.ds(at * PAIRS + s * 16, 16)
                cross_r[q, rows, cols] = (a * p + b * i).astype(jnp.bfloat16)
                cross_i[q, rows, cols] = (b * p - a * i).astype(jnp.bfloat16)

    for q in ORDER:
        two[q].wait_recv()
        sources[core, q] = second[q] + got2[q]
        hand[q].start()
        cross(q, 0)
    dims = (((1,), (1,)), ((), ()))
    for n, q in enumerate(ORDER):
        hand[q].wait_recv()
        cross(q, 1)
        sum_c = lax.dot_general(basis_c[q], cross_r[q], dims, preferred_element_type=jnp.float32)
        sum_s = lax.dot_general(basis_s[q], cross_i[q], dims, preferred_element_type=jnp.float32)
        if n == 0:
            acc_c[...] = sum_c
            acc_s[...] = sum_s
        else:
            acc_c[...] += sum_c
            acc_s[...] += sum_s

    window = (2 * me).astype(jnp.float32)
    scales = [1.0 + (window + at) * (1.0 / 128.0) for at in range(2)]
    for ahead in (True, False):
        start = 0 if ahead else 1
        c, s = acc_c[pl.ds(start, HALF), :], acc_s[pl.ds(start, HALF), :]
        lags = c + s if ahead else c - s
        halves = [(lags[:, w * PAIRS : (w + 1) * PAIRS] * scales[w]).reshape(32, BLOCK, PAIRS) for w in range(2)]
        both = jnp.concatenate(halves, axis=1).astype(jnp.bfloat16)
        if ahead:
            blocks[pl.ds(32, 32)] = both
        else:
            for m in range(32):
                blocks[31 - m] = both[m]
    pl.semaphore_wait(far, 2)
    for peer in peers:
        remote(blocks.at[peer], got.at[me], send_s, send_r, {"win": peer}).start()
    got[me] = blocks[me]
    wait_bytes(got.at[pl.ds(0, WIN - 1)], send_r)
    center = stack(got, vals)

    @pl.when(me >= 32)
    def _():
        o_ref[...] = center

    @pl.when(me < 32)
    def _():
        for k in range(BLOCK):
            o_ref[pl.ds(BLOCK - 1 - k, 1), :] = center[k : k + 1]

    wait_bytes(pair, pair_s)
    wait_bytes(first, one_s)
    wait_bytes(second, two_s)
    wait_bytes(sources.at[0], to_s)
    wait_bytes(blocks.at[pl.ds(0, WIN - 1)], send_s)


def per_device(spectra, source_channel):
    bf, f32, dma = jnp.bfloat16, jnp.float32, pltpu.SemaphoreType.DMA
    regular = pltpu.SemaphoreType.REGULAR
    result = pl.pallas_call(
        kernel,
        out_shape=jax.ShapeDtypeStruct((BLOCK, PAIRS), f32),
        in_specs=[pl.BlockSpec(memory_space=pltpu.HBM), pl.BlockSpec(memory_space=pltpu.HBM)],
        out_specs=pl.BlockSpec(memory_space=pltpu.VMEM),
        scratch_shapes=[
            pltpu.SMEM((8,), jnp.int32),
            pltpu.VMEM((NY, 2, 2, 16, QUARTER), bf),
            pltpu.VMEM((2, NY, 16, QUARTER), bf),
            *[pltpu.VMEM((NY, 16, QUARTER), bf) for _ in range(5)],
            pltpu.VMEM((2, NY, 16, QUARTER), bf),
            pltpu.VMEM((2, 16, QUARTER), f32),
            pltpu.VMEM((24, F), f32),
            pltpu.VMEM((24, F), f32),
            pltpu.VMEM((16, F), f32),
            pltpu.VMEM((16, F), f32),
            pltpu.VMEM((NY, ROWS, QUARTER), bf),
            pltpu.VMEM((NY, ROWS, QUARTER), bf),
            pltpu.VMEM((NY, 2 * PAIRS, QUARTER), bf),
            pltpu.VMEM((NY, 2 * PAIRS, QUARTER), bf),
            pltpu.VMEM((ROWS, 2 * PAIRS), f32),
            pltpu.VMEM((ROWS, 2 * PAIRS), f32),
            pltpu.VMEM((WIN, 2 * BLOCK, PAIRS), bf),
            pltpu.VMEM((WIN, 2 * BLOCK, PAIRS), bf),
            pltpu.VMEM((2 * WIN, BLOCK, PAIRS), f32),
            dma, dma((NY,)),
            dma, dma((NY,)), dma, dma((NY,)), dma, dma((NY,)), dma, dma((NY,)), dma, dma,
            regular, regular, regular,
        ],
        compiler_params=pltpu.CompilerParams(
            collective_id=0, has_side_effects=True, vmem_limit_bytes=40 * 1024 * 1024
        ),
    )(
        pltpu.with_memory_space_constraint(source_channel, pltpu.HBM),
        pltpu.with_memory_space_constraint(spectra, pltpu.HBM),
    )
    return result.reshape(BLOCK, 8, 16)


def solution(mesh):
    return jax.shard_map(
        per_device,
        mesh=mesh,
        in_specs=(P("win", None, "rcv", None), P()),
        out_specs=P("win", None, "rcv"),
        check_vma=False,
    )
```

```python
import jax
import jax.numpy as jnp
from jax import lax
from jax.experimental import pallas as pl
from jax.experimental.pallas import tpu as pltpu
from jax.sharding import PartitionSpec as P

L = 512
F = 4096
ITERS = 5
TUKEY = 4.685
EPSILON = 1e-06
MESH = pl.DeviceIdType.MESH
NZ, NX, NY = 16, 4, 4
WIN = NZ * NX
BLOCK = L // WIN
HALF = L // 2
ROWS = HALF + 16
PIECES = 4
PIECE = F // PIECES
ORDER = tuple(p for pair in zip(range(PIECES // 2), range(PIECES // 2, PIECES)) for p in pair)
COLS = 512
PAIRS = 128


def signed(step, count):
    return step if step <= count // 2 else step - count


def offsets():
    found = [(dz, dx) for dz in range(NZ) for dx in range(NX) if dz or dx]
    return sorted(found, key=lambda o: -(4 * abs(signed(o[0], NZ)) + abs(signed(o[1], NX))))


def cos_sin(phase):
    turn = (phase + 1024) >> 11
    x = (phase - (turn << 11)).astype(jnp.float32) * (2.0 * jnp.pi / (2 * F))
    y = x * x
    s = x * (1.0 + y * (-1.0 / 6 + y * (1.0 / 120 + y * (-1.0 / 5040 + y * (1.0 / 362880)))))
    c = 1.0 + y * (-0.5 + y * (1.0 / 24 + y * (-1.0 / 720 + y * (1.0 / 40320))))
    odd = (turn & 1) == 1
    cos = jnp.where(odd, s, c)
    sin = jnp.where(odd, c, s)
    cos = jnp.where(((turn + 1) & 2) == 2, -cos, cos)
    sin = jnp.where((turn & 2) == 2, -sin, sin)
    return cos, sin


def fill_table(cos_ref, sin_ref, rows, step, scaled):
    for part in range(F // COLS):
        cols = pl.ds(part * COLS, COLS)
        freq = part * COLS + lax.broadcasted_iota(jnp.int32, (rows, COLS), 1)
        row = lax.broadcasted_iota(jnp.int32, (rows, COLS), 0)
        cos, sin = cos_sin((row * freq * step) & (2 * F - 1))
        if scaled:
            factor = jnp.where(freq == 0, 1.0, 2.0) * (1.0 / (8 * F) ** 0.5)
            cos, sin = cos * factor, sin * factor
        cos_ref[:, cols] = cos
        sin_ref[:, cols] = sin


def fill_basis(first, last, coarse_c, coarse_s, fine_c, fine_s, basis_c, basis_s):
    for part in range(F // COLS):
        cols = pl.ds(part * COLS, COLS)
        piece, start = divmod(part * COLS, PIECE)
        fc, fs = fine_c[:, cols], fine_s[:, cols]

        def one(g, _, cols=cols, piece=piece, start=start, fc=fc, fs=fs):
            cc, cs = coarse_c[pl.ds(g, 1), cols], coarse_s[pl.ds(g, 1), cols]
            rows = pl.ds(pl.multiple_of(g * 16, 16), 16)
            basis_c[piece, rows, start : start + COLS] = (cc * fc - cs * fs).astype(jnp.bfloat16)
            basis_s[piece, rows, start : start + COLS] = (-(cs * fc) - cc * fs).astype(jnp.bfloat16)
            return 0

        lax.fori_loop(first, last, one, 0)


def read_half(got, vals, at):
    sums = [None] * 8
    for w in range(WIN):
        value = got[at, w].astype(jnp.float32) * (1.0 / (1.0 + (2 * w + at) / 128.0))
        vals[at * WIN + w] = value
        sums[w % 8] = value if sums[w % 8] is None else sums[w % 8] + value
    return sum(sums[1:], sums[0])


def stack(total, vals):
    windows = 2 * WIN
    mean = total * (1.0 / windows)
    sums = [jnp.zeros_like(mean)] * 8
    for w in range(windows):
        dev = vals[w] - mean
        sums[w % 8] = sums[w % 8] + dev * dev
    var = sum(sums[1:], sums[0]) * (1.0 / windows)
    center = mean
    for _ in range(ITERS):
        shift = mean - center
        inverse = 1.0 / (TUKEY * TUKEY * (var + shift * shift + EPSILON))
        weights = [jnp.zeros_like(mean)] * 8
        moved = [jnp.zeros_like(mean)] * 8
        for w in range(windows):
            dev = vals[w] - center
            root = jnp.maximum(1.0 - dev * dev * inverse, 0.0)
            weight = root * root
            weights[w % 8] = weights[w % 8] + weight
            moved[w % 8] = moved[w % 8] + weight * dev
        center = center + sum(moved[1:], moved[0]) / sum(weights[1:], weights[0])
    return center


def remote(src, dst, send_sem, recv_sem, where):
    return pltpu.make_async_remote_copy(src, dst, send_sem, recv_sem, device_id=where, device_id_type=MESH)


def wait_bytes(ref, sem):
    pltpu.make_async_copy(ref, ref, sem).wait()


def kernel(
    channel_hbm, spectra_ref, o_ref,
    channel_ref, spec, own, pair, first, got1, second, got2, sources, source_f,
    coarse_c, coarse_s, fine_c, fine_s, basis_c, basis_s, cross_r, cross_i, acc_c, acc_s,
    blocks, got, vals,
    chan_sem, spec_sem, pair_s, pair_r, one_s, one_r, two_s, two_r, to_s, to_r, send_s, send_r,
    know,
):
    me = lax.axis_index("win")
    z, x = me // NX, lax.rem(me, NX)
    mine = lax.axis_index("rcv")
    y, core = mine // 2, lax.rem(mine, 2)
    other = 1 - core

    def at_offset(dz, dx):
        return lax.rem(z + NZ + dz, NZ) * NX + lax.rem(x + NX + dx, NX)

    partner = {"rcv": 2 * y + other}
    left = {"rcv": 2 * (y + 1 - 2 * lax.rem(y, 2)) + core}
    right = {"rcv": 2 * (NY - 1 - y) + core}

    loads = {
        p: pltpu.make_async_copy(spectra_ref.at[:, :, :, pl.ds(p * PIECE, PIECE)], spec.at[p], spec_sem.at[p])
        for p in ORDER
    }
    for p in ORDER:
        loads[p].start()
    channels = pltpu.make_async_copy(channel_hbm, channel_ref, chan_sem)
    channels.start()
    barrier = pltpu.get_barrier_semaphore()
    steps = {0: ((0, -1), (0, 1)), 1: ((-1, 0), (1, 0)), 2: ((-2, 0), (2, 0)), 3: ((-4, 0), (4, 0)), 4: ((-1, 0), (1, 0))}
    for where in (partner, left, right):
        pl.semaphore_signal(barrier, inc=1, device_id=where, device_id_type=MESH)
    for offset in steps[0] + steps[1]:
        pl.semaphore_signal(barrier, inc=1, device_id={"win": at_offset(*offset)}, device_id_type=MESH)

    def tell(n):
        for offset in steps[n]:
            pl.semaphore_signal(know.at[n], inc=1, device_id={"win": at_offset(*offset)}, device_id_type=MESH)

    def learn(n):
        pl.semaphore_wait(know.at[n], 2)

    fill_table(fine_c, fine_s, 16, 1, False)
    fill_table(coarse_c, coarse_s, 24, 16, True)
    channels.wait()
    row = lax.broadcasted_iota(jnp.int32, (16, 16), 0)
    column = lax.broadcasted_iota(jnp.int32, (16, 16), 1) + mine * 16
    onehot = jnp.zeros((16, 16), jnp.float32)
    for s in range(8):
        onehot = jnp.where((row == s) & (column == channel_ref[s]), 1.0, onehot)
    onehot = onehot.astype(jnp.bfloat16)
    for p in ORDER:
        loads[p].wait()
    for w in range(2):
        for p in range(PIECES):
            picked = [
                jnp.dot(onehot, spec[p, w, c], preferred_element_type=jnp.float32)[:8] for c in range(2)
            ]
            own[w, p] = jnp.concatenate(picked, axis=0).astype(jnp.bfloat16)
    pl.semaphore_wait(barrier, 7)
    tell(0)

    half = PIECES // 2
    swap = {p: remote(own.at[other, p], pair.at[p], pair_s, pair_r.at[p], partner) for p in ORDER}
    one = {p: remote(first.at[p], got1.at[p], one_s, one_r.at[p], left if p < half else right) for p in ORDER}
    two = {p: remote(second.at[p], got2.at[p], two_s, two_r.at[p], right if p < half else left) for p in ORDER}
    hand = {p: remote(sources.at[core, p], sources.at[core, p], to_s, to_r.at[p], partner) for p in ORDER}
    for p in ORDER:
        swap[p].start()
    for p in ORDER:
        swap[p].wait_recv()
        first[p] = own[core, p] + pair[p]
        one[p].start()
    learn(0)
    tell(1)
    fill_basis(0, 8, coarse_c, coarse_s, fine_c, fine_s, basis_c, basis_s)
    learn(1)
    tell(2)
    fill_basis(8, ROWS // 16, coarse_c, coarse_s, fine_c, fine_s, basis_c, basis_s)
    for p in ORDER:
        one[p].wait_recv()
        second[p] = first[p] + got1[p]
        two[p].start()
    learn(2)
    tell(3)

    dims = (((1,), (1,)), ((), ()))

    def compute(n, p, at):
        w = other if at else core
        source_f[at] = sources[w, p].astype(jnp.float32)
        for part in range(PIECE // COLS):
            cols = pl.ds(part * COLS, COLS)
            re = spec[p, w, 0, :, cols].astype(jnp.float32)
            im = spec[p, w, 1, :, cols].astype(jnp.float32)
            for s in range(8):
                a = source_f[at, pl.ds(s, 1), cols]
                b = source_f[at, pl.ds(8 + s, 1), cols]
                rows = pl.ds(s * 16, 16)
                cross_r[at, p, rows, cols] = (a * re + b * im).astype(jnp.bfloat16)
                cross_i[at, p, rows, cols] = (b * re - a * im).astype(jnp.bfloat16)
        sum_c = lax.dot_general(basis_c[p], cross_r[at, p], dims, preferred_element_type=jnp.float32)
        sum_s = lax.dot_general(basis_s[p], cross_i[at, p], dims, preferred_element_type=jnp.float32)
        if n == 0:
            acc_c[at] = sum_c
            acc_s[at] = sum_s
        else:
            acc_c[at] += sum_c
            acc_s[at] += sum_s

    def send(at):
        scale = 1.0 + ((2 * me).astype(jnp.float32) + at) * (1.0 / 128.0)
        plus = acc_c[at, pl.ds(0, HALF), :] + acc_s[at, pl.ds(0, HALF), :]
        blocks[at, pl.ds(32, 32)] = (plus * scale).reshape(32, BLOCK, PAIRS).astype(jnp.bfloat16)
        minus = acc_c[at, pl.ds(1, HALF), :] - acc_s[at, pl.ds(1, HALF), :]
        minus = (minus * scale).reshape(32, BLOCK, PAIRS).astype(jnp.bfloat16)
        for m in range(32):
            blocks[at, 31 - m] = minus[m]
        if at == 0:
            learn(4)
        for dz, dx in offsets():
            peer = at_offset(dz, dx)
            remote(blocks.at[at, peer], got.at[at, me], send_s.at[at], send_r.at[at], {"win": peer}).start()
        got[at, me] = blocks[at, me]

    for n, p in enumerate(ORDER):
        two[p].wait_recv()
        sources[core, p] = second[p] + got2[p]
        hand[p].start()
        if n == PIECES - 1:
            learn(3)
            tell(4)
        compute(n, p, 0)
    send(0)
    for n, p in enumerate(ORDER):
        hand[p].wait_recv()
        compute(n, p, 1)
    send(1)
    most = pl.ds(0, WIN - 1)
    wait_bytes(got.at[0, most], send_r.at[0])
    total = read_half(got, vals, 0)
    wait_bytes(got.at[1, most], send_r.at[1])
    center = stack(total + read_half(got, vals, 1), vals)

    @pl.when(me >= 32)
    def _():
        o_ref[...] = center

    @pl.when(me < 32)
    def _():
        for k in range(BLOCK):
            o_ref[pl.ds(BLOCK - 1 - k, 1), :] = center[k : k + 1]

    wait_bytes(pair, pair_s)
    wait_bytes(first, one_s)
    wait_bytes(second, two_s)
    wait_bytes(sources.at[0], to_s)
    for at in range(2):
        wait_bytes(blocks.at[at, most], send_s.at[at])


def per_device(spectra, source_channel):
    bf, f32, dma = jnp.bfloat16, jnp.float32, pltpu.SemaphoreType.DMA
    result = pl.pallas_call(
        kernel,
        out_shape=jax.ShapeDtypeStruct((BLOCK, PAIRS), f32),
        in_specs=[pl.BlockSpec(memory_space=pltpu.HBM), pl.BlockSpec(memory_space=pltpu.HBM)],
        out_specs=pl.BlockSpec(memory_space=pltpu.VMEM),
        scratch_shapes=[
            pltpu.SMEM((8,), jnp.int32),
            pltpu.VMEM((PIECES, 2, 2, 16, PIECE), bf),
            pltpu.VMEM((2, PIECES, 16, PIECE), bf),
            *[pltpu.VMEM((PIECES, 16, PIECE), bf) for _ in range(5)],
            pltpu.VMEM((2, PIECES, 16, PIECE), bf),
            pltpu.VMEM((2, 16, PIECE), f32),
            pltpu.VMEM((24, F), f32),
            pltpu.VMEM((24, F), f32),
            pltpu.VMEM((16, F), f32),
            pltpu.VMEM((16, F), f32),
            pltpu.VMEM((PIECES, ROWS, PIECE), bf),
            pltpu.VMEM((PIECES, ROWS, PIECE), bf),
            pltpu.VMEM((2, PIECES, PAIRS, PIECE), bf),
            pltpu.VMEM((2, PIECES, PAIRS, PIECE), bf),
            pltpu.VMEM((2, ROWS, PAIRS), f32),
            pltpu.VMEM((2, ROWS, PAIRS), f32),
            pltpu.VMEM((2, WIN, BLOCK, PAIRS), bf),
            pltpu.VMEM((2, WIN, BLOCK, PAIRS), bf),
            pltpu.VMEM((2 * WIN, BLOCK, PAIRS), f32),
            dma, dma((PIECES,)),
            dma, dma((PIECES,)), dma, dma((PIECES,)), dma, dma((PIECES,)), dma, dma((PIECES,)),
            dma((2,)), dma((2,)),
            pltpu.SemaphoreType.REGULAR((5,)),
        ],
        compiler_params=pltpu.CompilerParams(
            collective_id=0, has_side_effects=True, vmem_limit_bytes=40 * 1024 * 1024
        ),
    )(
        pltpu.with_memory_space_constraint(source_channel, pltpu.HBM),
        pltpu.with_memory_space_constraint(spectra, pltpu.HBM),
    )
    return result.reshape(BLOCK, 8, 16)


def solution(mesh):
    return jax.shard_map(
        per_device,
        mesh=mesh,
        in_specs=(P("win", None, "rcv", None), P()),
        out_specs=P("win", None, "rcv"),
        check_vma=False,
    )
```

```python
import jax
import jax.numpy as jnp
from jax import lax
from jax.experimental import pallas as pl
from jax.experimental.pallas import tpu as pltpu
from jax.sharding import PartitionSpec as P

L = 512
F = 4096
ITERS = 5
TUKEY = 4.685
EPSILON = 1e-06
MESH = pl.DeviceIdType.MESH
NZ, NX, NY = 16, 4, 4
WIN = NZ * NX
BLOCK = L // WIN
HALF = L // 2
ROWS = HALF + 16
PIECES = 4
PIECE = F // PIECES


ORDER = tuple(p for pair in zip(range(PIECES // 2), range(PIECES // 2, PIECES)) for p in pair)
COLS = 512
PAIRS = 128
LAST = (NZ // 2, NX // 2)


def signed(step, count):
    return step if step <= count // 2 else step - count


def offsets():
    found = [(dz, dx) for dz in range(NZ) for dx in range(NX) if dz or dx]
    return sorted(found, key=lambda o: -(4 * abs(signed(o[0], NZ)) + abs(signed(o[1], NX))))


def cos_sin(phase):
    turn = (phase + 1024) >> 11
    x = (phase - (turn << 11)).astype(jnp.float32) * (2.0 * jnp.pi / (2 * F))
    y = x * x
    s = x * (1.0 + y * (-1.0 / 6 + y * (1.0 / 120 + y * (-1.0 / 5040 + y * (1.0 / 362880)))))
    c = 1.0 + y * (-0.5 + y * (1.0 / 24 + y * (-1.0 / 720 + y * (1.0 / 40320))))
    odd = (turn & 1) == 1
    cos = jnp.where(odd, s, c)
    sin = jnp.where(odd, c, s)
    cos = jnp.where(((turn + 1) & 2) == 2, -cos, cos)
    sin = jnp.where((turn & 2) == 2, -sin, sin)
    return cos, sin


def fill_table(cos_ref, sin_ref, rows, step, scaled):
    for part in range(F // COLS):
        cols = pl.ds(part * COLS, COLS)
        freq = part * COLS + lax.broadcasted_iota(jnp.int32, (rows, COLS), 1)
        row = lax.broadcasted_iota(jnp.int32, (rows, COLS), 0)
        cos, sin = cos_sin((row * freq * step) & (2 * F - 1))
        if scaled:
            factor = jnp.where(freq == 0, 1.0, 2.0) * (1.0 / (8 * F) ** 0.5)
            cos, sin = cos * factor, sin * factor
        cos_ref[:, cols] = cos
        sin_ref[:, cols] = sin


def fill_basis(first, last, coarse_c, coarse_s, fine_c, fine_s, basis_c, basis_s):
    for part in range(F // COLS):
        cols = pl.ds(part * COLS, COLS)
        piece, start = divmod(part * COLS, PIECE)
        fc, fs = fine_c[:, cols], fine_s[:, cols]

        def one(g, _, cols=cols, piece=piece, start=start, fc=fc, fs=fs):
            cc, cs = coarse_c[pl.ds(g, 1), cols], coarse_s[pl.ds(g, 1), cols]
            rows = pl.ds(pl.multiple_of(g * 16, 16), 16)
            basis_c[piece, rows, start : start + COLS] = (cc * fc - cs * fs).astype(jnp.bfloat16)
            basis_s[piece, rows, start : start + COLS] = (-(cs * fc) - cc * fs).astype(jnp.bfloat16)
            return 0

        lax.fori_loop(first, last, one, 0)


def fold(sums):
    return (sums[0] + sums[1]) + (sums[2] + sums[3]) + ((sums[4] + sums[5]) + (sums[6] + sums[7]))


def read_half(got, vals, at, origin):
    sums, squares = [0.0] * 8, [0.0] * 8
    for w in range(WIN):
        value = got[at, w].astype(jnp.float32) * (1.0 / (1.0 + (2 * w + at) / 128.0))
        if origin is None:
            origin = value
        value = value - origin
        vals[at * WIN + w] = value
        sums[w % 8] += value
        squares[w % 8] += value * value
    return origin, fold(sums), fold(squares)


def stack(total, squares, vals):
    windows = 2 * WIN
    mean = total * (1.0 / windows)
    var = jnp.maximum(squares * (1.0 / windows) - mean * mean, 0.0)
    center = mean
    for _ in range(ITERS):
        shift = mean - center
        inverse = 1.0 / (TUKEY * TUKEY * (var + shift * shift + EPSILON))
        weights, moved = [0.0] * 8, [0.0] * 8
        for w in range(windows):
            dev = vals[w] - center
            root = jnp.maximum(1.0 - dev * dev * inverse, 0.0)
            weight = root * root
            weights[w % 8] += weight
            moved[w % 8] += weight * dev
        center = center + fold(moved) / fold(weights)
    return center


def remote(src, dst, send_sem, recv_sem, where):
    return pltpu.make_async_remote_copy(src, dst, send_sem, recv_sem, device_id=where, device_id_type=MESH)


def wait_bytes(ref, sem):
    pltpu.make_async_copy(ref, ref, sem).wait()


def kernel(
    channel_hbm, spectra_ref, o_ref,
    channel_ref, spec, own, pair, first, got1, second, got2, sources, source_f,
    coarse_c, coarse_s, fine_c, fine_s, basis_c, basis_s, cross_r, cross_i, acc_c, acc_s,
    blocks, got, vals,
    chan_sem, spec_sem, pair_s, pair_r, one_s, one_r, two_s, two_r, to_s, to_r, send_s, send_r,
    know,
):
    me = lax.axis_index("win")
    z, x = me // NX, lax.rem(me, NX)
    mine = lax.axis_index("rcv")
    y, core = mine // 2, lax.rem(mine, 2)
    other = 1 - core

    def at_offset(dz, dx):
        return lax.rem(z + NZ + dz, NZ) * NX + lax.rem(x + NX + dx, NX)

    partner = {"rcv": 2 * y + other}
    left = {"rcv": 2 * (y + 1 - 2 * lax.rem(y, 2)) + core}
    right = {"rcv": 2 * (NY - 1 - y) + core}

    loads = {
        p: pltpu.make_async_copy(spectra_ref.at[:, :, :, pl.ds(p * PIECE, PIECE)], spec.at[p], spec_sem.at[p])
        for p in ORDER
    }
    for p in ORDER:
        loads[p].start()
    channels = pltpu.make_async_copy(channel_hbm, channel_ref, chan_sem)
    channels.start()
    barrier = pltpu.get_barrier_semaphore()
    steps = {0: ((0, -1), (0, 1)), 1: ((-1, 0), (1, 0)), 2: ((-2, 0), (2, 0)), 3: ((-4, 0), (4, 0)), 4: ((-1, 0), (1, 0))}
    for where in (partner, left, right):
        pl.semaphore_signal(barrier, inc=1, device_id=where, device_id_type=MESH)
    for offset in steps[0] + steps[1]:
        pl.semaphore_signal(barrier, inc=1, device_id={"win": at_offset(*offset)}, device_id_type=MESH)

    def tell(n):
        for offset in steps[n]:
            pl.semaphore_signal(know.at[n], inc=1, device_id={"win": at_offset(*offset)}, device_id_type=MESH)

    def learn(n):
        pl.semaphore_wait(know.at[n], 2)

    fill_table(fine_c, fine_s, 16, 1, False)
    fill_table(coarse_c, coarse_s, 24, 16, True)
    channels.wait()
    row = lax.broadcasted_iota(jnp.int32, (16, 16), 0)
    column = lax.broadcasted_iota(jnp.int32, (16, 16), 1) + mine * 16
    onehot = jnp.zeros((16, 16), jnp.float32)
    for s in range(8):
        onehot = jnp.where((row == s) & (column == channel_ref[s]), 1.0, onehot)
    onehot = onehot.astype(jnp.bfloat16)
    for p in ORDER:
        loads[p].wait()
    for w in range(2):
        for p in range(PIECES):
            picked = [
                jnp.dot(onehot, spec[p, w, c], preferred_element_type=jnp.float32)[:8] for c in range(2)
            ]
            own[w, p] = jnp.concatenate(picked, axis=0).astype(jnp.bfloat16)
    pl.semaphore_wait(barrier, 7)
    tell(0)

    half = PIECES // 2
    swap = {p: remote(own.at[other, p], pair.at[p], pair_s, pair_r.at[p], partner) for p in ORDER}
    one = {p: remote(first.at[p], got1.at[p], one_s, one_r.at[p], left if p < half else right) for p in ORDER}
    two = {p: remote(second.at[p], got2.at[p], two_s, two_r.at[p], right if p < half else left) for p in ORDER}
    hand = {p: remote(sources.at[core, p], sources.at[core, p], to_s, to_r.at[p], partner) for p in ORDER}
    for p in ORDER:
        swap[p].start()
    for p in ORDER:
        swap[p].wait_recv()
        first[p] = own[core, p] + pair[p]
        one[p].start()
    learn(0)
    tell(1)
    fill_basis(0, 8, coarse_c, coarse_s, fine_c, fine_s, basis_c, basis_s)
    learn(1)
    tell(2)
    for p in ORDER:
        one[p].wait_recv()
        second[p] = first[p] + got1[p]
        two[p].start()
    learn(2)
    tell(3)
    fill_basis(8, ROWS // 16, coarse_c, coarse_s, fine_c, fine_s, basis_c, basis_s)

    dims = (((1,), (1,)), ((), ()))

    def compute(n, p, at):
        w = other if at else core
        source_f[at] = sources[w, p].astype(jnp.float32)
        for part in range(PIECE // COLS):
            cols = pl.ds(part * COLS, COLS)
            re = spec[p, w, 0, :, cols].astype(jnp.float32)
            im = spec[p, w, 1, :, cols].astype(jnp.float32)
            for s in range(8):
                a = source_f[at, pl.ds(s, 1), cols]
                b = source_f[at, pl.ds(8 + s, 1), cols]
                rows = pl.ds(s * 16, 16)
                cross_r[at, p, rows, cols] = (a * re + b * im).astype(jnp.bfloat16)
                cross_i[at, p, rows, cols] = (b * re - a * im).astype(jnp.bfloat16)
        sum_c = lax.dot_general(basis_c[p], cross_r[at, p], dims, preferred_element_type=jnp.float32)
        sum_s = lax.dot_general(basis_s[p], cross_i[at, p], dims, preferred_element_type=jnp.float32)
        if n == 0:
            acc_c[at] = sum_c
            acc_s[at] = sum_s
        else:
            acc_c[at] += sum_c
            acc_s[at] += sum_s

    def send(at):
        scale = 1.0 + ((2 * me).astype(jnp.float32) + at) * (1.0 / 128.0)
        plus = acc_c[at, pl.ds(0, HALF), :] + acc_s[at, pl.ds(0, HALF), :]
        blocks[at, pl.ds(32, 32)] = (plus * scale).reshape(32, BLOCK, PAIRS).astype(jnp.bfloat16)
        minus = acc_c[at, pl.ds(1, HALF), :] - acc_s[at, pl.ds(1, HALF), :]
        minus = (minus * scale).reshape(32, BLOCK, PAIRS).astype(jnp.bfloat16)
        for m in range(32):
            blocks[at, 31 - m] = minus[m]
        if at:
            learn(4)
        for half in range(at + 1):
            for dz, dx in offsets():
                if half != at and (dz, dx) != LAST or half == at == 0 and (dz, dx) == LAST:
                    continue
                peer = at_offset(dz, dx)
                there = got.at[half, me]
                remote(blocks.at[half, peer], there, send_s.at[half], send_r.at[half], {"win": peer}).start()
        got[at, me] = blocks[at, me]

    for n, p in enumerate(ORDER):
        two[p].wait_recv()
        sources[core, p] = second[p] + got2[p]
        hand[p].start()
        if n == PIECES - 1:
            learn(3)
            tell(4)
        compute(n, p, 0)
    send(0)
    for n, p in enumerate(ORDER):
        hand[p].wait_recv()
        compute(n, p, 1)
    send(1)
    most = pl.ds(0, WIN - 1)
    wait_bytes(got.at[0, most], send_r.at[0])
    origin, total0, squares0 = read_half(got, vals, 0, None)
    wait_bytes(got.at[1, most], send_r.at[1])
    _, total1, squares1 = read_half(got, vals, 1, origin)
    center = origin + stack(total0 + total1, squares0 + squares1, vals)

    @pl.when(me >= 32)
    def _():
        o_ref[...] = center

    @pl.when(me < 32)
    def _():
        for k in range(BLOCK):
            o_ref[pl.ds(BLOCK - 1 - k, 1), :] = center[k : k + 1]

    wait_bytes(pair, pair_s)
    wait_bytes(first, one_s)
    wait_bytes(second, two_s)
    wait_bytes(sources.at[0], to_s)
    for at in range(2):
        wait_bytes(blocks.at[at, most], send_s.at[at])


def per_device(spectra, source_channel):
    bf, f32, dma = jnp.bfloat16, jnp.float32, pltpu.SemaphoreType.DMA
    result = pl.pallas_call(
        kernel,
        out_shape=jax.ShapeDtypeStruct((BLOCK, PAIRS), f32),
        in_specs=[pl.BlockSpec(memory_space=pltpu.HBM), pl.BlockSpec(memory_space=pltpu.HBM)],
        out_specs=pl.BlockSpec(memory_space=pltpu.VMEM),
        scratch_shapes=[
            pltpu.SMEM((8,), jnp.int32),
            pltpu.VMEM((PIECES, 2, 2, 16, PIECE), bf),
            pltpu.VMEM((2, PIECES, 16, PIECE), bf),
            *[pltpu.VMEM((PIECES, 16, PIECE), bf) for _ in range(5)],
            pltpu.VMEM((2, PIECES, 16, PIECE), bf),
            pltpu.VMEM((2, 16, PIECE), f32),
            pltpu.VMEM((24, F), f32),
            pltpu.VMEM((24, F), f32),
            pltpu.VMEM((16, F), f32),
            pltpu.VMEM((16, F), f32),
            pltpu.VMEM((PIECES, ROWS, PIECE), bf),
            pltpu.VMEM((PIECES, ROWS, PIECE), bf),
            pltpu.VMEM((2, PIECES, PAIRS, PIECE), bf),
            pltpu.VMEM((2, PIECES, PAIRS, PIECE), bf),
            pltpu.VMEM((2, ROWS, PAIRS), f32),
            pltpu.VMEM((2, ROWS, PAIRS), f32),
            pltpu.VMEM((2, WIN, BLOCK, PAIRS), bf),
            pltpu.VMEM((2, WIN, BLOCK, PAIRS), bf),
            pltpu.VMEM((2 * WIN, BLOCK, PAIRS), f32),
            dma, dma((PIECES,)),
            dma, dma((PIECES,)), dma, dma((PIECES,)), dma, dma((PIECES,)), dma, dma((PIECES,)),
            dma((2,)), dma((2,)),
            pltpu.SemaphoreType.REGULAR((5,)),
        ],
        compiler_params=pltpu.CompilerParams(
            collective_id=0, has_side_effects=True, vmem_limit_bytes=40 * 1024 * 1024
        ),
    )(
        pltpu.with_memory_space_constraint(source_channel, pltpu.HBM),
        pltpu.with_memory_space_constraint(spectra, pltpu.HBM),
    )
    return result.reshape(BLOCK, 8, 16)


def solution(mesh):
    return jax.shard_map(
        per_device,
        mesh=mesh,
        in_specs=(P("win", None, "rcv", None), P()),
        out_specs=P("win", None, "rcv"),
        check_vma=False,
    )
```

```python
import jax
import jax.numpy as jnp
from jax import lax
from jax.experimental import pallas as pl
from jax.experimental.pallas import tpu as pltpu
from jax.sharding import PartitionSpec as P

L = 512
F = 4096
ITERS = 5
TUKEY = 4.685
EPSILON = 1e-06
MESH = pl.DeviceIdType.MESH
NZ, NX, NY = 16, 4, 4
WIN = NZ * NX
BLOCK = L // WIN
HALF = L // 2
ROWS = HALF + 16
PIECES = 4
PIECE = F // PIECES


ORDER = tuple(p for pair in zip(range(PIECES // 2), range(PIECES // 2, PIECES)) for p in pair)
COLS = 512
PAIRS = 128
LAST = (NZ // 2, NX // 2)


def signed(step, count):
    return step if step <= count // 2 else step - count


def offsets():
    found = [(dz, dx) for dz in range(NZ) for dx in range(NX) if dz or dx]
    return sorted(found, key=lambda o: -(4 * abs(signed(o[0], NZ)) + abs(signed(o[1], NX))))


def cos_sin(phase):
    turn = (phase + 1024) >> 11
    x = (phase - (turn << 11)).astype(jnp.float32) * (2.0 * jnp.pi / (2 * F))
    y = x * x
    s = x * (1.0 + y * (-1.0 / 6 + y * (1.0 / 120 + y * (-1.0 / 5040 + y * (1.0 / 362880)))))
    c = 1.0 + y * (-0.5 + y * (1.0 / 24 + y * (-1.0 / 720 + y * (1.0 / 40320))))
    odd = (turn & 1) == 1
    cos = jnp.where(odd, s, c)
    sin = jnp.where(odd, c, s)
    cos = jnp.where(((turn + 1) & 2) == 2, -cos, cos)
    sin = jnp.where((turn & 2) == 2, -sin, sin)
    return cos, sin


def fill_table(cos_ref, sin_ref, rows, step, scaled):
    for part in range(F // COLS):
        cols = pl.ds(part * COLS, COLS)
        freq = part * COLS + lax.broadcasted_iota(jnp.int32, (rows, COLS), 1)
        row = lax.broadcasted_iota(jnp.int32, (rows, COLS), 0)
        cos, sin = cos_sin((row * freq * step) & (2 * F - 1))
        if scaled:
            factor = jnp.where(freq == 0, 1.0, 2.0) * (1.0 / (8 * F) ** 0.5)
            cos, sin = cos * factor, sin * factor
        cos_ref[:, cols] = cos
        sin_ref[:, cols] = sin


def fill_basis(first, last, coarse_c, coarse_s, fine_c, fine_s, basis_c, basis_s):
    for part in range(F // COLS):
        cols = pl.ds(part * COLS, COLS)
        piece, start = divmod(part * COLS, PIECE)
        fc, fs = fine_c[:, cols], fine_s[:, cols]

        def one(g, _, cols=cols, piece=piece, start=start, fc=fc, fs=fs):
            cc, cs = coarse_c[pl.ds(g, 1), cols], coarse_s[pl.ds(g, 1), cols]
            rows = pl.ds(pl.multiple_of(g * 16, 16), 16)
            basis_c[piece, rows, start : start + COLS] = (cc * fc - cs * fs).astype(jnp.bfloat16)
            basis_s[piece, rows, start : start + COLS] = (-(cs * fc) - cc * fs).astype(jnp.bfloat16)
            return 0

        lax.fori_loop(first, last, one, 0)


def fold(sums):
    return (sums[0] + sums[1]) + (sums[2] + sums[3]) + ((sums[4] + sums[5]) + (sums[6] + sums[7]))


def read_half(got, vals, at, origin):
    sums, squares = [0.0] * 8, [0.0] * 8
    for w in range(WIN):
        value = got[at, w].astype(jnp.float32) * (1.0 / (1.0 + (2 * w + at) / 128.0))
        if origin is None:
            origin = value
        value = value - origin
        vals[at * WIN + w] = value
        sums[w % 8] += value
        squares[w % 8] += value * value
    return origin, fold(sums), fold(squares)


def stack(total, squares, vals):
    windows = 2 * WIN
    mean = total * (1.0 / windows)
    var = jnp.maximum(squares * (1.0 / windows) - mean * mean, 0.0)
    center = mean
    for _ in range(ITERS):
        shift = mean - center
        inverse = 1.0 / (TUKEY * TUKEY * (var + shift * shift + EPSILON))
        weights, moved = [0.0] * 8, [0.0] * 8
        for w in range(windows):
            dev = vals[w] - center
            root = jnp.maximum(1.0 - dev * dev * inverse, 0.0)
            weight = root * root
            weights[w % 8] += weight
            moved[w % 8] += weight * dev
        center = center + fold(moved) / fold(weights)
    return center


def remote(src, dst, send_sem, recv_sem, where):
    return pltpu.make_async_remote_copy(src, dst, send_sem, recv_sem, device_id=where, device_id_type=MESH)


def wait_bytes(ref, sem):
    pltpu.make_async_copy(ref, ref, sem).wait()


def kernel(
    channel_hbm, spectra_ref, o_ref,
    channel_ref, spec, own, pair, first, got1, second, got2, sources, source_f,
    coarse_c, coarse_s, fine_c, fine_s, basis_c, basis_s, cross_r, cross_i, acc_c, acc_s,
    blocks, got, vals,
    chan_sem, spec_sem, pair_s, pair_r, one_s, one_r, two_s, two_r, to_s, to_r, send_s, send_r,
    know,
):
    me = lax.axis_index("win")
    z, x = me // NX, lax.rem(me, NX)
    mine = lax.axis_index("rcv")
    y, core = mine // 2, lax.rem(mine, 2)
    other = 1 - core

    def at_offset(dz, dx):
        return lax.rem(z + NZ + dz, NZ) * NX + lax.rem(x + NX + dx, NX)

    partner = {"rcv": 2 * y + other}
    left = {"rcv": 2 * (y + 1 - 2 * lax.rem(y, 2)) + core}
    right = {"rcv": 2 * (NY - 1 - y) + core}

    loads = {
        p: pltpu.make_async_copy(spectra_ref.at[:, :, :, pl.ds(p * PIECE, PIECE)], spec.at[p], spec_sem.at[p])
        for p in ORDER
    }
    for p in ORDER:
        loads[p].start()
    channels = pltpu.make_async_copy(channel_hbm, channel_ref, chan_sem)
    channels.start()
    barrier = pltpu.get_barrier_semaphore()
    steps = {0: ((0, -1), (0, 1)), 1: ((-1, 0), (1, 0)), 2: ((-2, 0), (2, 0)), 3: ((-4, 0), (4, 0)), 4: ((-1, 0), (1, 0))}
    for where in (partner, left, right):
        pl.semaphore_signal(barrier, inc=1, device_id=where, device_id_type=MESH)
    for offset in steps[0] + steps[1]:
        pl.semaphore_signal(barrier, inc=1, device_id={"win": at_offset(*offset)}, device_id_type=MESH)

    def tell(n):
        for offset in steps[n]:
            pl.semaphore_signal(know.at[n], inc=1, device_id={"win": at_offset(*offset)}, device_id_type=MESH)

    def learn(n):
        pl.semaphore_wait(know.at[n], 2)

    fill_table(fine_c, fine_s, 16, 1, False)
    fill_table(coarse_c, coarse_s, 24, 16, True)
    channels.wait()
    row = lax.broadcasted_iota(jnp.int32, (16, 16), 0)
    column = lax.broadcasted_iota(jnp.int32, (16, 16), 1) + mine * 16
    onehot = jnp.zeros((16, 16), jnp.float32)
    for s in range(8):
        onehot = jnp.where((row == s) & (column == channel_ref[s]), 1.0, onehot)
    onehot = onehot.astype(jnp.bfloat16)
    for p in ORDER:
        loads[p].wait()

    def pick(at):
        for p in ORDER:
            picked = [
                jnp.dot(onehot, spec[p, other if at else core, c], preferred_element_type=jnp.float32)[:8]
                for c in range(2)
            ]
            own[at, p] = jnp.concatenate(picked, axis=0).astype(jnp.bfloat16)

    pick(1)
    pl.semaphore_wait(barrier, 7)
    tell(0)

    half = PIECES // 2
    swap = {p: remote(own.at[1, p], pair.at[p], pair_s, pair_r.at[p], partner) for p in ORDER}
    one = {p: remote(first.at[p], got1.at[p], one_s, one_r.at[p], left if p < half else right) for p in ORDER}
    two = {p: remote(second.at[p], got2.at[p], two_s, two_r.at[p], right if p < half else left) for p in ORDER}
    hand = {p: remote(sources.at[core, p], sources.at[core, p], to_s, to_r.at[p], partner) for p in ORDER}
    for p in ORDER:
        swap[p].start()
    pick(0)
    for p in ORDER:
        swap[p].wait_recv()
        first[p] = own[0, p] + pair[p]
        one[p].start()
    learn(0)
    tell(1)
    fill_basis(0, 8, coarse_c, coarse_s, fine_c, fine_s, basis_c, basis_s)
    learn(1)
    tell(2)
    for p in ORDER:
        one[p].wait_recv()
        second[p] = first[p] + got1[p]
        two[p].start()
    learn(2)
    tell(3)
    fill_basis(8, ROWS // 16, coarse_c, coarse_s, fine_c, fine_s, basis_c, basis_s)

    dims = (((1,), (1,)), ((), ()))

    def compute(n, p, at):
        w = other if at else core
        source_f[at] = sources[w, p].astype(jnp.float32)
        for part in range(PIECE // COLS):
            cols = pl.ds(part * COLS, COLS)
            re = spec[p, w, 0, :, cols].astype(jnp.float32)
            im = spec[p, w, 1, :, cols].astype(jnp.float32)
            for s in range(8):
                a = source_f[at, pl.ds(s, 1), cols]
                b = source_f[at, pl.ds(8 + s, 1), cols]
                rows = pl.ds(s * 16, 16)
                cross_r[at, p, rows, cols] = (a * re + b * im).astype(jnp.bfloat16)
                cross_i[at, p, rows, cols] = (b * re - a * im).astype(jnp.bfloat16)
        sum_c = lax.dot_general(basis_c[p], cross_r[at, p], dims, preferred_element_type=jnp.float32)
        sum_s = lax.dot_general(basis_s[p], cross_i[at, p], dims, preferred_element_type=jnp.float32)
        if n == 0:
            acc_c[at] = sum_c
            acc_s[at] = sum_s
        else:
            acc_c[at] += sum_c
            acc_s[at] += sum_s

    def send(at):
        scale = 1.0 + ((2 * me).astype(jnp.float32) + at) * (1.0 / 128.0)
        plus = acc_c[at, pl.ds(0, HALF), :] + acc_s[at, pl.ds(0, HALF), :]
        blocks[at, pl.ds(32, 32)] = (plus * scale).reshape(32, BLOCK, PAIRS).astype(jnp.bfloat16)
        minus = acc_c[at, pl.ds(1, HALF), :] - acc_s[at, pl.ds(1, HALF), :]
        minus = (minus * scale).reshape(32, BLOCK, PAIRS).astype(jnp.bfloat16)
        for m in range(32):
            blocks[at, 31 - m] = minus[m]
        if at:
            learn(4)
        for half in range(at + 1):
            for dz, dx in offsets():
                if half != at and (dz, dx) != LAST or half == at == 0 and (dz, dx) == LAST:
                    continue
                peer = at_offset(dz, dx)
                there = got.at[half, me]
                remote(blocks.at[half, peer], there, send_s.at[half], send_r.at[half], {"win": peer}).start()
        got[at, me] = blocks[at, me]

    for n, p in enumerate(ORDER):
        two[p].wait_recv()
        sources[core, p] = second[p] + got2[p]
        hand[p].start()
        if n == PIECES - 1:
            learn(3)
            tell(4)
        compute(n, p, 0)
    send(0)
    for n, p in enumerate(ORDER):
        hand[p].wait_recv()
        compute(n, p, 1)
    send(1)
    most = pl.ds(0, WIN - 1)
    wait_bytes(got.at[0, most], send_r.at[0])
    origin, total0, squares0 = read_half(got, vals, 0, None)
    wait_bytes(got.at[1, most], send_r.at[1])
    _, total1, squares1 = read_half(got, vals, 1, origin)
    center = origin + stack(total0 + total1, squares0 + squares1, vals)

    @pl.when(me >= 32)
    def _():
        o_ref[...] = center

    @pl.when(me < 32)
    def _():
        for k in range(BLOCK):
            o_ref[pl.ds(BLOCK - 1 - k, 1), :] = center[k : k + 1]

    wait_bytes(pair, pair_s)
    wait_bytes(first, one_s)
    wait_bytes(second, two_s)
    wait_bytes(sources.at[0], to_s)
    for at in range(2):
        wait_bytes(blocks.at[at, most], send_s.at[at])


def per_device(spectra, source_channel):
    bf, f32, dma = jnp.bfloat16, jnp.float32, pltpu.SemaphoreType.DMA
    result = pl.pallas_call(
        kernel,
        out_shape=jax.ShapeDtypeStruct((BLOCK, PAIRS), f32),
        in_specs=[pl.BlockSpec(memory_space=pltpu.HBM), pl.BlockSpec(memory_space=pltpu.HBM)],
        out_specs=pl.BlockSpec(memory_space=pltpu.VMEM),
        scratch_shapes=[
            pltpu.SMEM((8,), jnp.int32),
            pltpu.VMEM((PIECES, 2, 2, 16, PIECE), bf),
            pltpu.VMEM((2, PIECES, 16, PIECE), bf),
            *[pltpu.VMEM((PIECES, 16, PIECE), bf) for _ in range(5)],
            pltpu.VMEM((2, PIECES, 16, PIECE), bf),
            pltpu.VMEM((2, 16, PIECE), f32),
            pltpu.VMEM((24, F), f32),
            pltpu.VMEM((24, F), f32),
            pltpu.VMEM((16, F), f32),
            pltpu.VMEM((16, F), f32),
            pltpu.VMEM((PIECES, ROWS, PIECE), bf),
            pltpu.VMEM((PIECES, ROWS, PIECE), bf),
            pltpu.VMEM((2, PIECES, PAIRS, PIECE), bf),
            pltpu.VMEM((2, PIECES, PAIRS, PIECE), bf),
            pltpu.VMEM((2, ROWS, PAIRS), f32),
            pltpu.VMEM((2, ROWS, PAIRS), f32),
            pltpu.VMEM((2, WIN, BLOCK, PAIRS), bf),
            pltpu.VMEM((2, WIN, BLOCK, PAIRS), bf),
            pltpu.VMEM((2 * WIN, BLOCK, PAIRS), f32),
            dma, dma((PIECES,)),
            dma, dma((PIECES,)), dma, dma((PIECES,)), dma, dma((PIECES,)), dma, dma((PIECES,)),
            dma((2,)), dma((2,)),
            pltpu.SemaphoreType.REGULAR((5,)),
        ],
        compiler_params=pltpu.CompilerParams(
            collective_id=0, has_side_effects=True, vmem_limit_bytes=40 * 1024 * 1024
        ),
    )(
        pltpu.with_memory_space_constraint(source_channel, pltpu.HBM),
        pltpu.with_memory_space_constraint(spectra, pltpu.HBM),
    )
    return result.reshape(BLOCK, 8, 16)


def solution(mesh):
    return jax.shard_map(
        per_device,
        mesh=mesh,
        in_specs=(P("win", None, "rcv", None), P()),
        out_specs=P("win", None, "rcv"),
        check_vma=False,
    )
```
